32 devices in a mesh: member: 4 (over y, x), group: 8 (over z, core).
Axes of the slice: x: 2, y: 2, z: 4, core: 2. Of those that a mesh axis runs over, the one named last changes fastest.
Arguments:
- agg_one: bfloat16 [16384, 768], P(('member', 'group')), may hold values from -6 to 6
- agg_two: bfloat16 [16384, 768], P(('member', 'group')), may hold values from -6 to 6
- grad_out: bfloat16 [16384, 768], P(('member', 'group')), may hold values from -6 to 6
- hop_one_weight: bfloat16 [768, 768], replicated, may hold values from -0.21875 to 0.21875
- hop_two_weight: bfloat16 [768, 768], replicated, may hold values from -0.21875 to 0.21875
- block_values: bfloat16 [768, 256, 256], P(('member', 'group')), may hold values from 0 to 0.046875
- src_slot: int32 [32, 24], P(('member', 'group')), may hold values from 0 to 13, as said below
- dst_block: int32 [32, 24], P(('member', 'group')), may hold values from 0 to 1
- block_count: int32 [32], P(('member', 'group')), may hold values from 9 to 24, as said below
- send_member: int32 [32, 4, 1], P(('member', 'group')), may hold values from 0 to 1, as said below
- send_group: int32 [32, 8], P(('member', 'group')), may hold values from 0 to 1, as said below
Outputs:
- grad_emb: bfloat16 [16384, 768], P(('member', 'group'))
- grad_w_one: float32 [768, 768], replicated
- grad_w_two: float32 [768, 768], replicated
The draws below stay inside these ranges and needn't reach their ends.
Inputs may be any that keep to these rules, and one draw needn't show every extreme that they name: `send_member`: for device d, entry [d, p, 0] is the label block of d, counted within d, sent to the device of member index p in d's group; one for every p. `send_group`: entry [d, h] is the label block of d, counted within d, sent to the device of group h with d's member index; one for every h. The first block_count[d] slots of device d are live, the rest hold 0 in src_slot and dst_block and are not read; some device has all 24 slots live. `src_slot`: encodes the source block as in the reference program. For device d of group g, slot j < 8 - 1 holds 2 + 4 + ((g + 1 + j) % 8); every later slot holds a value under 2 + 4.
All inputs are finite; a program needn't handle non-finite values.
Results may differ from the reference program's by a relative error of at most 0.0065.
Values may be sent and summed in bfloat16 or wider, within the bound.
No kernel may reach another device: no remote copies, remote signals or barrier semaphores. Data moves between devices by JAX's collectives and lax.ppermute only.
A program may use at most 128 MiB of HBM per device.

```python
import jax
import jax.numpy as jnp
from jax import lax

D = 768
BLK = 256
RB = 2
MCAP = 1
NBS = 24
NRB = 64
LABELS = 16384
N_MEMBER = 4
N_GROUP = 8
DEVICES = 32


def graph_tables(key):
    base = jax.random.fold_in(key, 7001)
    keys = jax.random.split(base, 9)
    scores = jax.random.randint(keys[0], (DEVICES, N_MEMBER, RB), 0, 1 << 20) * RB + jnp.arange(RB, dtype=jnp.int32)
    ordered = jnp.argsort(scores, axis=-1, stable=True)
    send_member = ordered[:, :, :MCAP].astype(jnp.int32)
    send_group = jax.random.randint(keys[1], (DEVICES, N_GROUP), 0, RB).astype(jnp.int32)
    counts = jax.random.randint(keys[2], (DEVICES,), N_GROUP - 1 + RB, NBS + 1)
    full_device = jax.random.randint(keys[3], (), 0, DEVICES)
    counts = jnp.where(jnp.arange(DEVICES, dtype=jnp.int32) == full_device, NBS, counts).astype(jnp.int32)
    kinds = jax.random.randint(keys[4], (DEVICES, NBS), 0, 10)
    local_pick = jax.random.randint(keys[5], (DEVICES, NBS), 0, RB)
    member_pick = jax.random.randint(keys[6], (DEVICES, NBS), 0, N_MEMBER * MCAP)
    own_group = (jnp.arange(DEVICES, dtype=jnp.int32) % N_GROUP)[:, None]
    slot_pos = jnp.arange(NBS, dtype=jnp.int32)[None, :]
    cross_pick = (own_group + 1 + slot_pos) % N_GROUP
    slot_ids = jnp.where(slot_pos < N_GROUP - 1, RB + N_MEMBER * MCAP + cross_pick, jnp.where(kinds < 4, local_pick, RB + member_pick))
    live_mask = slot_pos < counts[:, None]
    slot_ids = jnp.where(live_mask, slot_ids, 0).astype(jnp.int32)
    targets = jnp.where(live_mask, jax.random.randint(keys[8], (DEVICES, NBS), 0, RB), 0).astype(jnp.int32)
    return (send_member, send_group, counts, slot_ids, targets)


def draw_send_member(key, part):
    return graph_tables(key)[0]


def draw_send_group(key, part):
    return graph_tables(key)[1]


def draw_block_count(key, part):
    return graph_tables(key)[2]


def draw_src_slot(key, part):
    return graph_tables(key)[3]


def draw_dst_block(key, part):
    return graph_tables(key)[4]


def block_levels(rng, dims, shards, smallest, top_value):
    def one(dim, blocks):
        heights = jax.random.uniform(jax.random.fold_in(jax.random.fold_in(rng, 6), dim), (blocks,), jnp.float32, smallest / len(shards), top_value / len(shards))
        return jnp.repeat(jnp.exp(heights), dims[dim] // blocks).reshape((-1,) + (1,) * (len(dims) - dim - 1))

    gain = one(*shards[0])
    for cut in shards[1:]:
        gain = gain * one(*cut)
    return gain


def bell_draw(key, shape, spread, limit, cuts=(), kind=jnp.bfloat16):
    level = block_levels(key, shape, cuts, -0.22, 0.18) if cuts else 1.0
    array = jax.random.normal(key, shape, jnp.float32) * spread * level
    return jnp.minimum(jnp.maximum(array, -limit), limit).astype(kind)


def setup_inputs(seed: int = 0) -> dict:
    streams_of = jax.random.split(jax.random.key(seed), 12)
    agg_one = bell_draw(streams_of[0], (LABELS, D), 1.0, 6.0, ((0, 32),))
    agg_two = bell_draw(streams_of[1], (LABELS, D), 1.0, 6.0, ((0, 32),))
    grad_out = bell_draw(streams_of[2], (LABELS, D), 1.0, 6.0, ((0, 32),))
    hop_one_weight = bell_draw(streams_of[3], (D, D), D ** -0.5, 0.21875)
    hop_two_weight = bell_draw(streams_of[4], (D, D), D ** -0.5, 0.21875)
    block_values = jnp.clip(0.046875 * jax.random.uniform(streams_of[5], (DEVICES * NBS, BLK, BLK), jnp.float32) ** block_levels(streams_of[5], (DEVICES * NBS, BLK, BLK), ((0, 32),), -0.2, 0.2), 0.0, 0.046875).astype(jnp.bfloat16)
    src_slot = draw_src_slot(jax.random.fold_in(streams_of[11], 71), 0)
    dst_block = draw_dst_block(jax.random.fold_in(streams_of[11], 71), 0)
    block_count = draw_block_count(jax.random.fold_in(streams_of[11], 71), 0)
    send_member = draw_send_member(jax.random.fold_in(streams_of[11], 71), 0)
    send_group = draw_send_group(jax.random.fold_in(streams_of[11], 71), 0)
    return dict(agg_one=agg_one, agg_two=agg_two, grad_out=grad_out, hop_one_weight=hop_one_weight, hop_two_weight=hop_two_weight, block_values=block_values, src_slot=src_slot, dst_block=dst_block, block_count=block_count, send_member=send_member, send_group=send_group)


def silu_slope(value):
    sig = jax.nn.sigmoid(value)
    return sig * (1.0 + value * (1.0 - sig))


def transposed_aggregate(field, block_values, src_slot, dst_block, block_count, send_member, send_group):
    all_blocks = field.reshape(NRB, BLK, D)

    def one_device(device):
        member_pos = device // N_GROUP
        group_pos = device % N_GROUP
        slot_ids = src_slot[device]
        member_off = jnp.clip(slot_ids - RB, 0, N_MEMBER * MCAP - 1)
        peer_member = member_off // MCAP
        slot_in_peer = member_off % MCAP
        peer_device = peer_member * N_GROUP + group_pos
        member_pick = send_member[peer_device, member_pos, slot_in_peer]
        cross_group = jnp.clip(slot_ids - RB - N_MEMBER * MCAP, 0, N_GROUP - 1)
        cross_device = member_pos * N_GROUP + cross_group
        cross_pick = send_group[cross_device, group_pos]
        source_block = jnp.where(slot_ids < RB, device * RB + slot_ids,
                                 jnp.where(slot_ids < RB + N_MEMBER * MCAP, peer_device * RB + member_pick,
                                           cross_device * RB + cross_pick)).astype(jnp.int32)
        pieces = all_blocks[source_block].astype(jnp.float32)
        block_vals = lax.dynamic_slice_in_dim(block_values, (device * NBS).astype(jnp.int32), NBS, 0).astype(jnp.float32)
        live_mask = jnp.arange(NBS, dtype=jnp.int32) < block_count[device]
        one_hot = ((dst_block[device][:, None] == jnp.arange(RB, dtype=jnp.int32)[None, :]) & live_mask[:, None]).astype(jnp.float32)
        products = jnp.einsum('kab,kad->kbd', block_vals, pieces)
        return jnp.einsum('kr,kbd->rbd', one_hot, products)

    summed = lax.map(one_device, jnp.arange(DEVICES, dtype=jnp.int32))
    return summed.reshape(LABELS, D)


def reference(agg_one, agg_two, grad_out, hop_one_weight, hop_two_weight, block_values, src_slot, dst_block, block_count, send_member, send_group):
    grad_scale = float(LABELS) ** -0.5
    lift_one = jnp.dot(agg_one, hop_one_weight, preferred_element_type=jnp.float32)
    lift_two = jnp.dot(agg_two, hop_two_weight, preferred_element_type=jnp.float32)
    pull_two = (grad_out.astype(jnp.float32) * silu_slope(lift_two)).astype(jnp.bfloat16)
    grad_w_two = jnp.dot(agg_two.T, pull_two, preferred_element_type=jnp.float32) * grad_scale
    back_two = jnp.dot(pull_two, hop_two_weight.T, preferred_element_type=jnp.float32).astype(jnp.bfloat16)
    carry_grad = grad_out.astype(jnp.float32) + transposed_aggregate(back_two, block_values, src_slot, dst_block, block_count, send_member, send_group)
    pull_one = (carry_grad * silu_slope(lift_one)).astype(jnp.bfloat16)
    grad_w_one = jnp.dot(agg_one.T, pull_one, preferred_element_type=jnp.float32) * grad_scale
    back_one = jnp.dot(pull_one, hop_one_weight.T, preferred_element_type=jnp.float32).astype(jnp.bfloat16)
    grad_emb = (carry_grad + transposed_aggregate(back_one, block_values, src_slot, dst_block, block_count, send_member, send_group)).astype(jnp.bfloat16)
    return (grad_emb, grad_w_one, grad_w_two)
```

```python
import functools

import jax
import jax.numpy as jnp
from jax import lax
from jax.experimental import pallas as pl
from jax.experimental.pallas import tpu as pltpu
from jax.sharding import PartitionSpec as P


F32 = jnp.float32
BF16 = jnp.bfloat16
VMEM = pl.BlockSpec(memory_space=pltpu.VMEM)
SMEM = pl.BlockSpec(memory_space=pltpu.SMEM)
ANY = pl.BlockSpec(memory_space=pl.ANY)
LIMIT = 48 << 20


def silu_slope(value):
    sig = jax.nn.sigmoid(value)
    return sig * (1.0 + value * (1.0 - sig))


def turned_dot(values, rows):
    return lax.dot_general(values, rows, (((0,), (0,)), ((), ())), preferred_element_type=F32)


def times_transpose(left, weight):
    return lax.dot_general(left, weight, (((1,), (1,)), ((), ())), preferred_element_type=F32)


def start_sends(back, send_group, send_member, group_outs, member_outs, sems, rows):
    groups = send_group.shape[1]
    members, capacity = send_member.shape[1], send_member.shape[2]
    own_group, own_member = lax.axis_index("group"), lax.axis_index("member")
    copies = []

    def send(block, out):
        source = back.at[pl.ds(pl.multiple_of(block * rows, rows), rows), :]
        copies.append(pltpu.make_async_copy(source, out, sems.at[len(copies)]))
        copies[-1].start()

    for slot, out in enumerate(group_outs):
        send(send_group[0, lax.rem(own_group + (2 * groups - 1 - slot), groups)], out)
    for place, out in enumerate(member_outs):
        shift, which = 1 + place // capacity, place % capacity
        send(send_member[0, lax.rem(own_member + shift, members), which], out)
    return copies


def first_kernel(rows, cross, send_group, send_member, agg, weight, grad, pull_out, back_out, *rest):
    *outs, sems = rest
    for start in range(0, agg.shape[0], rows):
        part = pl.ds(start, rows)
        lift = jnp.dot(agg[part, :], weight[...], preferred_element_type=F32)
        pull = (grad[part, :].astype(F32) * silu_slope(lift)).astype(BF16)
        pull_out[part, :] = pull
        back_out[part, :] = times_transpose(pull, weight[...]).astype(BF16)
    for copy in start_sends(back_out, send_group, send_member, outs[:cross], outs[cross:], sems, rows):
        copy.wait()


def sweep_kernel(rows, cross, src_slot, dst_block, block_count, send_member, back, base, values, *rest):
    *received, total, pool, sems = rest
    members, capacity = send_member.shape[1], send_member.shape[2]
    local = back.shape[0] // rows
    own = lax.axis_index("member")
    copies = []

    def fill(source, slot):
        copies.append(pltpu.make_async_copy(source, pool.at[slot], sems.at[len(copies)]))
        copies[-1].start()

    for block in range(local):
        fill(back.at[pl.ds(block * rows, rows), :], block)
    for which in range(capacity):
        block = send_member[0, own, which]
        fill(back.at[pl.ds(pl.multiple_of(block * rows, rows), rows), :], local + own * capacity + which)
    for place, source in enumerate(received):
        shift, which = 1 + place // capacity, place % capacity
        peer = lax.rem(own + (members - shift), members)
        fill(source, local + peer * capacity + which)
    total[...] = base[...].astype(F32).reshape(total.shape)
    for copy in copies:
        copy.wait()

    def step(slot, carry):
        total[dst_block[0, slot]] += turned_dot(values[slot], pool[src_slot[0, slot]])
        return carry

    lax.fori_loop(cross, block_count[0], step, 0)


def fetch(copies, sems):
    started = [pltpu.make_async_copy(source, to, sems.at[i]) for i, (source, to) in enumerate(copies)]
    for copy in started:
        copy.start()
    return started


def add_cross(total, dst_block, held, blocks, loads):
    for slot, (load_values, load_block) in enumerate(zip(loads[0::2], loads[1::2])):
        load_values.wait()
        load_block.wait()
        total[dst_block[0, slot]] += turned_dot(held[slot], blocks[slot])


def cross_pairs(values, held, received, blocks):
    pairs = []
    for slot, source in enumerate(received):
        pairs += [(values.at[slot], held.at[slot]), (source, blocks.at[slot])]
    return pairs


def middle_kernel(rows, cross, send_group, send_member, dst_block, base, slope, weight, values, *rest):
    received, rest = rest[:cross], rest[cross:]
    carry_out, pull_out, back_out, *outs, held, blocks, slope_in, weight_in, sems, send_sems = rest
    pairs = [(base, carry_out)] + cross_pairs(values, held, received, blocks)
    first, *loads, load_slope, load_weight = fetch(pairs + [(slope, slope_in), (weight, weight_in)], sems)
    first.wait()
    add_cross(carry_out, dst_block, held, blocks, loads)
    load_slope.wait()
    load_weight.wait()
    for block in range(carry_out.shape[0]):
        part = pl.ds(block * rows, rows)
        pull = (carry_out[block] * slope_in[part, :]).astype(BF16)
        pull_out[part, :] = pull
        back_out[part, :] = times_transpose(pull, weight_in[...]).astype(BF16)
    for copy in start_sends(back_out, send_group, send_member, outs[:cross], outs[cross:], send_sems, rows):
        copy.wait()


def last_kernel(rows, cross, dst_block, base, values, *rest):
    received, (out, total, held, blocks, sems) = rest[:cross], rest[cross:]
    first, *loads = fetch([(base, total)] + cross_pairs(values, held, received, blocks), sems)
    first.wait()
    add_cross(total, dst_block, held, blocks, loads)
    out[...] = total[...].reshape(out.shape).astype(BF16)


def params():
    return pltpu.CompilerParams(vmem_limit_bytes=LIMIT)


def send_shapes(rows, width, count):
    return [jax.ShapeDtypeStruct((rows, width), BF16)] * count


def exchange(group_sends, member_sends, capacity):
    groups, members = lax.axis_size("group"), lax.axis_size("member")
    from_group = [
        lax.ppermute(block, "group", [((g + 1 + slot) % groups, g) for g in range(groups)])
        for slot, block in enumerate(group_sends)
    ]
    from_member = [
        lax.ppermute(block, "member", [(m, (m + 1 + place // capacity) % members) for m in range(members)])
        for place, block in enumerate(member_sends)
    ]
    return from_group, from_member


def stage_peers(axis, stride, size):
    total = lax.axis_size(axis)

    def moved(index, shift):
        place = index // stride % size
        return index + ((place + shift) % size - place) * stride

    perms = [[(i, moved(i, shift)) for i in range(total)] for shift in range(1, size)]
    return lax.axis_index(axis) // stride % size, perms


def weight_total(part):
    groups, members = lax.axis_size("group"), lax.axis_size("member")
    pair = 2 if groups % 2 == 0 else 1
    stages = [("group", 1, pair), ("member", 1, members), ("group", pair, groups // pair)]
    stages = [stage for stage in stages if stage[2] > 1]
    for axis, stride, size in stages:
        place, perms = stage_peers(axis, stride, size)
        pieces = part.reshape(size, part.shape[0] // size, part.shape[1])

        def piece(shift):
            return lax.dynamic_index_in_dim(pieces, (place + shift) % size, 0, keepdims=False)

        got = [
            lax.ppermute(piece(shift).astype(BF16), axis, perm) for shift, perm in enumerate(perms, 1)
        ]
        part = sum((block.astype(F32) for block in got), piece(0))
    part = part.astype(BF16)
    for axis, stride, size in reversed(stages):
        place, perms = stage_peers(axis, stride, size)
        whole = jnp.zeros((size,) + part.shape, BF16)
        whole = lax.dynamic_update_index_in_dim(whole, part, place, 0)
        for shift, perm in enumerate(perms, 1):
            block = lax.ppermute(part, axis, perm)
            whole = lax.dynamic_update_index_in_dim(whole, block, (place - shift) % size, 0)
        part = whole.reshape(size * part.shape[0], part.shape[1])
    return part.astype(F32)


def weight_part(aggregate, pulled):
    return lax.dot_general(aggregate, pulled, (((0,), (0,)), ((), ())), preferred_element_type=F32)


def body(
    agg_one,
    agg_two,
    grad_out,
    hop_one_weight,
    hop_two_weight,
    block_values,
    src_slot,
    dst_block,
    block_count,
    send_member,
    send_group,
):
    groups, members = lax.axis_size("group"), lax.axis_size("member")
    labels, width = agg_one.shape
    slots, rows = block_values.shape[:2]
    local = labels // rows
    capacity = send_member.shape[2]
    cross = groups - 1
    peers = (members - 1) * capacity
    grad_scale = float(labels * members * groups) ** (-0.5)

    field = jax.ShapeDtypeStruct((labels, width), BF16)
    total = jax.ShapeDtypeStruct((local, rows, width), F32)
    sends = send_shapes(rows, width, cross + peers)
    send_sems = pltpu.SemaphoreType.DMA((cross + peers,))
    cross_scratch = [
        pltpu.VMEM((cross, rows, rows), BF16),
        pltpu.VMEM((cross, rows, width), BF16),
    ]

    def sweep(back, base, received):
        return pl.pallas_call(
            functools.partial(sweep_kernel, rows, cross),
            out_shape=total,
            in_specs=[SMEM, SMEM, SMEM, SMEM, ANY, VMEM, VMEM] + [ANY] * peers,
            out_specs=VMEM,
            scratch_shapes=[
                pltpu.VMEM((local + members * capacity, rows, width), BF16),
                pltpu.SemaphoreType.DMA((local + members * capacity,)),
            ],
            compiler_params=params(),
            name="sweep",
        )(src_slot, dst_block, block_count, send_member, back, base, block_values, *received)

    pull_two, back_two, *outs = pl.pallas_call(
        functools.partial(first_kernel, rows, cross),
        out_shape=[field, field] + sends,
        in_specs=[SMEM, SMEM, VMEM, VMEM, VMEM],
        out_specs=[VMEM, VMEM] + [ANY] * (cross + peers),
        scratch_shapes=[send_sems],
        compiler_params=params(),
        name="first",
    )(send_group, send_member, agg_two, hop_two_weight, grad_out)
    from_group, from_member = exchange(outs[:cross], outs[cross:], capacity)

    slope_one = silu_slope(jnp.dot(agg_one, hop_one_weight, preferred_element_type=F32))
    grad_w_two = weight_total(weight_part(agg_two, pull_two)) * grad_scale
    base_two = sweep(back_two, grad_out, from_member)

    carry, pull_one, back_one, *outs = pl.pallas_call(
        functools.partial(middle_kernel, rows, cross),
        out_shape=[total, field, field] + sends,
        in_specs=[SMEM, SMEM, SMEM] + [ANY] * (4 + cross),
        out_specs=[VMEM, VMEM, VMEM] + [ANY] * (cross + peers),
        scratch_shapes=cross_scratch
        + [
            pltpu.VMEM((labels, width), F32),
            pltpu.VMEM(hop_one_weight.shape, BF16),
            pltpu.SemaphoreType.DMA((2 * cross + 3,)),
            send_sems,
        ],
        compiler_params=params(),
        name="middle",
    )(send_group, send_member, dst_block, base_two, slope_one, hop_one_weight, block_values, *from_group)
    from_group, from_member = exchange(outs[:cross], outs[cross:], capacity)

    grad_w_one = weight_total(weight_part(agg_one, pull_one)) * grad_scale
    base_one = sweep(back_one, carry, from_member)

    grad_emb = pl.pallas_call(
        functools.partial(last_kernel, rows, cross),
        out_shape=field,
        in_specs=[SMEM] + [ANY] * (2 + cross),
        out_specs=VMEM,
        scratch_shapes=[pltpu.VMEM((local, rows, width), F32)]
        + cross_scratch
        + [pltpu.SemaphoreType.DMA((2 * cross + 1,))],
        compiler_params=params(),
        name="last",
    )(dst_block, base_one, block_values, *from_group)
    return (grad_emb, grad_w_one, grad_w_two)


def solution(mesh):
    in_specs = (
        P(("member", "group"), None),
        P(("member", "group"), None),
        P(("member", "group"), None),
        P(),
        P(),
        P(("member", "group"), None, None),
        P(("member", "group"), None),
        P(("member", "group"), None),
        P(("member", "group")),
        P(("member", "group"), None, None),
        P(("member", "group"), None),
    )
    out_specs = (P(("member", "group"), None), P(), P())
    return jax.shard_map(body, mesh=mesh, in_specs=in_specs, out_specs=out_specs, check_vma=False)
```

```python
import functools

import jax
import jax.numpy as jnp
from jax import lax
from jax.experimental import pallas as pl
from jax.experimental.pallas import tpu as pltpu
from jax.sharding import PartitionSpec as P


F32 = jnp.float32
BF16 = jnp.bfloat16
VMEM = pl.BlockSpec(memory_space=pltpu.VMEM)
SMEM = pl.BlockSpec(memory_space=pltpu.SMEM)
ANY = pl.BlockSpec(memory_space=pl.ANY)
LIMIT = 48 << 20
PAIR = 2


def silu_slope(value):
    sig = jax.nn.sigmoid(value)
    return sig * (1.0 + value * (1.0 - sig))


def turned_dot(values, rows):
    return lax.dot_general(values, rows, (((0,), (0,)), ((), ())), preferred_element_type=F32)


def times_transpose(left, weight):
    return lax.dot_general(left, weight, (((1,), (1,)), ((), ())), preferred_element_type=F32)


def start_sends(back, send_group, send_member, group_outs, member_outs, sems, rows):
    members, capacity = send_member.shape[1], send_member.shape[2]
    own_group, own_member = lax.axis_index("group"), lax.axis_index("member")
    copies = []

    def send(block, out):
        source = back.at[pl.ds(pl.multiple_of(block * rows, rows), rows), :]
        copies.append(pltpu.make_async_copy(source, out, sems.at[len(copies)]))
        copies[-1].start()

    for place, out in enumerate(group_outs):
        send(send_group[0, own_group ^ (place + 1)], out)
    for place, out in enumerate(member_outs):
        shift, which = 1 + place // capacity, place % capacity
        send(send_member[0, lax.rem(own_member + shift, members), which], out)
    return copies


def first_kernel(rows, cross, send_group, send_member, agg, weight, grad, pull_out, back_out, *rest):
    *outs, sems = rest
    for start in range(0, agg.shape[0], rows):
        part = pl.ds(start, rows)
        lift = jnp.dot(agg[part, :], weight[...], preferred_element_type=F32)
        pull = (grad[part, :].astype(F32) * silu_slope(lift)).astype(BF16)
        pull_out[part, :] = pull
        back_out[part, :] = times_transpose(pull, weight[...]).astype(BF16)
    for copy in start_sends(back_out, send_group, send_member, outs[:cross], outs[cross:], sems, rows):
        copy.wait()


def sweep_kernel(rows, cross, src_slot, dst_block, block_count, send_member, back, base, values, *rest):
    *received, total, pool, sems = rest
    members, capacity = send_member.shape[1], send_member.shape[2]
    local = back.shape[0] // rows
    own = lax.axis_index("member")
    copies = []

    def fill(source, slot):
        copies.append(pltpu.make_async_copy(source, pool.at[slot], sems.at[len(copies)]))
        copies[-1].start()

    for block in range(local):
        fill(back.at[pl.ds(block * rows, rows), :], block)
    for which in range(capacity):
        block = send_member[0, own, which]
        fill(back.at[pl.ds(pl.multiple_of(block * rows, rows), rows), :], local + own * capacity + which)
    for place, source in enumerate(received):
        shift, which = 1 + place // capacity, place % capacity
        peer = lax.rem(own + (members - shift), members)
        fill(source, local + peer * capacity + which)
    total[...] = base[...].astype(F32).reshape(total.shape)
    for copy in copies:
        copy.wait()

    def step(slot, carry):
        total[dst_block[0, slot]] += turned_dot(values[slot], pool[src_slot[0, slot]])
        return carry

    lax.fori_loop(cross, block_count[0], step, 0)


def is_inner(groups):
    chip = lax.axis_index("group") // PAIR
    return (chip > 0) & (chip < groups // PAIR - 1)


def fetch_cross(rows, groups, far_table, received, blocks, values, held, sems):
    own = lax.axis_index("group")
    loads = []

    def load(source, to):
        copy = pltpu.make_async_copy(source, to, sems.at[len(loads)])
        loads.append(copy)
        return copy

    for place, sources in enumerate(received):
        slot = lax.rem((own ^ (place + 1)) + (groups - 1 - own), groups)
        load(values.at[slot], held.at[place]).start()
        if len(sources) == 1:
            load(sources[0], blocks.at[place]).start()
            continue
        inner, outer = sources
        if inner.shape[0] != rows:
            picked = pl.multiple_of(far_table[0, own] * rows, rows)
            inner = inner.at[pl.ds(picked, rows), :]
        near = pltpu.make_async_copy(inner, blocks.at[place], sems.at[len(loads)])
        copy = load(outer, blocks.at[place])
        deep = is_inner(groups)

        @pl.when(deep)
        def _():
            near.start()

        @pl.when(jnp.logical_not(deep))
        def _():
            copy.start()

    return loads


def add_cross(groups, total, dst_block, held, blocks, loads):
    own = lax.axis_index("group")
    for place in range(groups - 1):
        slot = lax.rem((own ^ (place + 1)) + (groups - 1 - own), groups)
        loads[2 * place].wait()
        loads[2 * place + 1].wait()
        total[dst_block[0, slot]] += turned_dot(held[place], blocks[place])


def split_received(plan, refs):
    received = []
    for count in plan:
        received.append(refs[:count])
        refs = refs[count:]
    return received, refs


def relay_kernel(rows, far_table, raw, *rest):
    *outs, sems = rest
    own = lax.axis_index("group")
    copies = []
    for i, (peer, out) in enumerate(zip((1, 2, 3), outs)):
        block = far_table[0, own ^ peer]
        source = raw.at[pl.ds(pl.multiple_of(block * rows, rows), rows), :]
        copies.append(pltpu.make_async_copy(source, out, sems.at[i]))
        copies[-1].start()
    for copy in copies:
        copy.wait()


def middle_kernel(
    rows, plan, send_group, send_member, dst_block, far_table, base, slope, weight, values, after, *rest
):
    received, rest = split_received(plan, rest)
    cross = len(plan)
    carry_out, pull_out, back_out, *outs, held, blocks, sems, send_sems = rest
    loads = fetch_cross(rows, cross + 1, far_table, received, blocks, values, held, sems)
    carry_out[...] = base[...]
    add_cross(cross + 1, carry_out, dst_block, held, blocks, loads)
    for block in range(carry_out.shape[0]):
        part = pl.ds(block * rows, rows)
        pull = (carry_out[block] * slope[part, :]).astype(BF16)
        pull_out[part, :] = pull
        back_out[part, :] = times_transpose(pull, weight[...]).astype(BF16)
    for copy in start_sends(back_out, send_group, send_member, outs[:cross], outs[cross:], send_sems, rows):
        copy.wait()


def last_kernel(rows, plan, dst_block, far_table, base, values, after, *rest):
    received, (out, total, held, blocks, sems) = split_received(plan, rest)
    loads = fetch_cross(rows, len(plan) + 1, far_table, received, blocks, values, held, sems)
    total[...] = base[...]
    add_cross(len(plan) + 1, total, dst_block, held, blocks, loads)
    out[...] = total[...].reshape(out.shape).astype(BF16)


def params():
    return pltpu.CompilerParams(vmem_limit_bytes=LIMIT)


def send_shapes(rows, width, count):
    return [jax.ShapeDtypeStruct((rows, width), BF16)] * count


def relayed(groups):
    return groups == 4 * PAIR


def group_exchange(rows, back, group_sends, far_table):
    groups = lax.axis_size("group")
    line = relayed(groups)

    def inner(g):
        return 0 < g // PAIR < groups // PAIR - 1

    def permute(block, peer, keep=lambda g: True):
        return lax.ppermute(block, "group", [(g, g ^ peer) for g in range(groups) if keep(g)])

    if not line:
        return [[permute(block, peer)] for peer, block in enumerate(group_sends, 1)]
    raw = permute(back, 6, inner)
    near = {peer: permute(group_sends[peer - 1], peer) for peer in (2, 3)}
    far = {peer: permute(group_sends[peer - 1], peer, lambda g: not inner(g)) for peer in (6, 7, 4, 5)}
    sibling = permute(group_sends[0], 1)
    to_sibling, to_same, to_cross = pl.pallas_call(
        functools.partial(relay_kernel, rows),
        out_shape=send_shapes(rows, back.shape[1], 3),
        in_specs=[SMEM, ANY],
        out_specs=[ANY] * 3,
        scratch_shapes=[pltpu.SemaphoreType.DMA((3,))],
        compiler_params=params(),
        name="relay_pick",
    )(far_table, raw)
    same = permute(to_same, 2, inner)
    cross = permute(to_cross, 3, inner)
    swapped = permute(to_sibling, 1, inner)
    return [
        [sibling],
        [near[2]],
        [near[3]],
        [far[4], same],
        [far[5], cross],
        [raw, far[6]],
        [swapped, far[7]],
    ]


def member_exchange(member_sends, capacity):
    members = lax.axis_size("member")
    return [
        lax.ppermute(block, "member", [(m, (m + 1 + place // capacity) % members) for m in range(members)])
        for place, block in enumerate(member_sends)
    ]


def stage_peers(axis, stride, size):
    total = lax.axis_size(axis)

    def moved(index, shift):
        place = index // stride % size
        return index + ((place + shift) % size - place) * stride

    perms = [[(i, moved(i, shift)) for i in range(total)] for shift in range(1, size)]
    return lax.axis_index(axis) // stride % size, perms


def weight_total(part):
    groups, members = lax.axis_size("group"), lax.axis_size("member")
    stages = [("group", 1, PAIR), ("member", 1, members), ("group", PAIR, groups // PAIR)]
    for axis, stride, size in stages:
        place, perms = stage_peers(axis, stride, size)
        pieces = part.reshape(size, part.shape[0] // size, part.shape[1])

        def piece(shift):
            return lax.dynamic_index_in_dim(pieces, (place + shift) % size, 0, keepdims=False)

        got = [
            lax.ppermute(piece(shift).astype(BF16), axis, perm) for shift, perm in enumerate(perms, 1)
        ]
        part = sum((block.astype(F32) for block in got), piece(0))
    part = part.astype(BF16)
    for axis, stride, size in reversed(stages):
        place, perms = stage_peers(axis, stride, size)
        whole = jnp.zeros((size,) + part.shape, BF16)
        whole = lax.dynamic_update_index_in_dim(whole, part, place, 0)
        for shift, perm in enumerate(perms, 1):
            block = lax.ppermute(part, axis, perm)
            whole = lax.dynamic_update_index_in_dim(whole, block, (place - shift) % size, 0)
        part = whole.reshape(size * part.shape[0], part.shape[1])
    return part.astype(F32)


def weight_part(aggregate, pulled):
    return lax.dot_general(aggregate, pulled, (((0,), (0,)), ((), ())), preferred_element_type=F32)


def body(
    agg_one,
    agg_two,
    grad_out,
    hop_one_weight,
    hop_two_weight,
    block_values,
    src_slot,
    dst_block,
    block_count,
    send_member,
    send_group,
):
    groups, members = lax.axis_size("group"), lax.axis_size("member")
    labels, width = agg_one.shape
    _, rows = block_values.shape[:2]
    local = labels // rows
    capacity = send_member.shape[2]
    cross = groups - 1
    peers = (members - 1) * capacity
    grad_scale = float(labels * members * groups) ** (-0.5)

    field = jax.ShapeDtypeStruct((labels, width), BF16)
    total = jax.ShapeDtypeStruct((local, rows, width), F32)
    sends = send_shapes(rows, width, cross + peers)
    send_sems = pltpu.SemaphoreType.DMA((cross + peers,))
    cross_scratch = [
        pltpu.VMEM((cross, rows, rows), BF16),
        pltpu.VMEM((cross, rows, width), BF16),
    ]

    def sweep(back, base, received):
        return pl.pallas_call(
            functools.partial(sweep_kernel, rows, cross),
            out_shape=total,
            in_specs=[SMEM, SMEM, SMEM, SMEM, ANY, VMEM, VMEM] + [ANY] * peers,
            out_specs=VMEM,
            scratch_shapes=[
                pltpu.VMEM((local + members * capacity, rows, width), BF16),
                pltpu.SemaphoreType.DMA((local + members * capacity,)),
            ],
            compiler_params=params(),
            name="sweep",
        )(src_slot, dst_block, block_count, send_member, back, base, block_values, *received)

    far_table = send_group
    if relayed(groups):
        far_table = lax.ppermute(send_group, "group", [(g, g ^ 6) for g in range(groups)])
    plan = [1, 1, 1, 2, 2, 2, 2] if relayed(groups) else [1] * cross

    pull_two, back_two, *outs = pl.pallas_call(
        functools.partial(first_kernel, rows, cross),
        out_shape=[field, field] + sends,
        in_specs=[SMEM, SMEM, VMEM, VMEM, VMEM],
        out_specs=[VMEM, VMEM] + [ANY] * (cross + peers),
        scratch_shapes=[send_sems],
        compiler_params=params(),
        name="first",
    )(send_group, send_member, agg_two, hop_two_weight, grad_out)
    from_group = group_exchange(rows, back_two, outs[:cross], far_table)
    from_member = member_exchange(outs[cross:], capacity)
    slope_one = silu_slope(jnp.dot(agg_one, hop_one_weight, preferred_element_type=F32))
    grad_w_two = weight_total(weight_part(agg_two, pull_two)) * grad_scale
    base_two = sweep(back_two, grad_out, from_member)

    carry, pull_one, back_one, *outs = pl.pallas_call(
        functools.partial(middle_kernel, rows, plan),
        out_shape=[total, field, field] + sends,
        in_specs=[SMEM] * 4 + [VMEM] * 3 + [ANY] * (2 + sum(plan)),
        out_specs=[VMEM, VMEM, VMEM] + [ANY] * (cross + peers),
        scratch_shapes=cross_scratch + [pltpu.SemaphoreType.DMA((2 * cross,)), send_sems],
        compiler_params=params(),
        name="middle",
    )(
        *(send_group, send_member, dst_block, far_table, base_two, slope_one),
        *(hop_one_weight, block_values, grad_w_two),
        *sum(from_group, []),
    )
    from_group = group_exchange(rows, back_one, outs[:cross], far_table)
    from_member = member_exchange(outs[cross:], capacity)
    grad_w_one = weight_total(weight_part(agg_one, pull_one)) * grad_scale
    base_one = sweep(back_one, carry, from_member)

    grad_emb = pl.pallas_call(
        functools.partial(last_kernel, rows, plan),
        out_shape=field,
        in_specs=[SMEM] * 2 + [VMEM] + [ANY] * (2 + sum(plan)),
        out_specs=VMEM,
        scratch_shapes=[pltpu.VMEM((local, rows, width), F32)]
        + cross_scratch
        + [pltpu.SemaphoreType.DMA((2 * cross,))],
        compiler_params=params(),
        name="last",
    )(dst_block, far_table, base_one, block_values, grad_w_one, *sum(from_group, []))
    return (grad_emb, grad_w_one, grad_w_two)


def solution(mesh):
    in_specs = (
        P(("member", "group"), None),
        P(("member", "group"), None),
        P(("member", "group"), None),
        P(),
        P(),
        P(("member", "group"), None, None),
        P(("member", "group"), None),
        P(("member", "group"), None),
        P(("member", "group")),
        P(("member", "group"), None, None),
        P(("member", "group"), None),
    )
    out_specs = (P(("member", "group"), None), P(), P())
    return jax.shard_map(body, mesh=mesh, in_specs=in_specs, out_specs=out_specs, check_vma=False)
```

```python
import functools

import jax
import jax.numpy as jnp
from jax import lax
from jax.experimental import pallas as pl
from jax.experimental.pallas import tpu as pltpu
from jax.sharding import PartitionSpec as P


F32 = jnp.float32
BF16 = jnp.bfloat16
VMEM = pl.BlockSpec(memory_space=pltpu.VMEM)
SMEM = pl.BlockSpec(memory_space=pltpu.SMEM)
ANY = pl.BlockSpec(memory_space=pl.ANY)
LIMIT = 20 << 20
PAIR = 2


def silu_slope(value):
    sig = jax.nn.sigmoid(value)
    return sig * (1.0 + value * (1.0 - sig))


def turned_dot(values, rows):
    return lax.dot_general(values, rows, (((0,), (0,)), ((), ())), preferred_element_type=F32)


def times_transpose(left, weight):
    return lax.dot_general(left, weight, (((1,), (1,)), ((), ())), preferred_element_type=F32)


def start_sends(back, send_group, send_member, group_outs, member_outs, sems, rows):
    members, capacity = send_member.shape[1], send_member.shape[2]
    own_group, own_member = lax.axis_index("group"), lax.axis_index("member")
    copies = []

    def send(block, out):
        source = back.at[pl.ds(pl.multiple_of(block * rows, rows), rows), :]
        copies.append(pltpu.make_async_copy(source, out, sems.at[len(copies)]))
        copies[-1].start()

    for place, out in enumerate(group_outs):
        send(send_group[0, own_group ^ (place + 1)], out)
    for place, out in enumerate(member_outs):
        shift, which = 1 + place // capacity, place % capacity
        send(send_member[0, lax.rem(own_member + shift, members), which], out)
    return copies


def first_kernel(rows, cross, send_group, send_member, agg, weight, grad, pull_out, back_out, *rest):
    *outs, sems = rest
    for start in range(0, agg.shape[0], rows):
        part = pl.ds(start, rows)
        lift = jnp.dot(agg[part, :], weight[...], preferred_element_type=F32)
        pull = (grad[part, :].astype(F32) * silu_slope(lift)).astype(BF16)
        pull_out[part, :] = pull
        back_out[part, :] = times_transpose(pull, weight[...]).astype(BF16)
    for copy in start_sends(back_out, send_group, send_member, outs[:cross], outs[cross:], sems, rows):
        copy.wait()


def sweep_kernel(rows, cross, src_slot, dst_block, block_count, send_member, back, base, values, *rest):
    *received, total, pool, sems = rest
    members, capacity = send_member.shape[1], send_member.shape[2]
    local = back.shape[0] // rows
    own = lax.axis_index("member")
    copies = []

    def fill(source, slot):
        copies.append(pltpu.make_async_copy(source, pool.at[slot], sems.at[len(copies)]))
        copies[-1].start()

    for block in range(local):
        fill(back.at[pl.ds(block * rows, rows), :], block)
    for which in range(capacity):
        block = send_member[0, own, which]
        fill(back.at[pl.ds(pl.multiple_of(block * rows, rows), rows), :], local + own * capacity + which)
    for place, source in enumerate(received):
        shift, which = 1 + place // capacity, place % capacity
        peer = lax.rem(own + (members - shift), members)
        fill(source, local + peer * capacity + which)
    total[...] = base[...].astype(F32).reshape(total.shape)
    for copy in copies:
        copy.wait()

    def step(slot, carry):
        total[dst_block[0, slot]] += turned_dot(values[slot], pool[src_slot[0, slot]])
        return carry

    lax.fori_loop(cross, block_count[0], step, 0)


def is_inner(groups):
    chip = lax.axis_index("group") // PAIR
    return (chip > 0) & (chip < groups // PAIR - 1)


def fetch_cross(rows, groups, far_table, received, blocks, values, held, sems):
    own = lax.axis_index("group")
    loads = []

    def load(source, to):
        copy = pltpu.make_async_copy(source, to, sems.at[len(loads)])
        loads.append(copy)
        return copy

    for place, sources in enumerate(received):
        slot = lax.rem((own ^ (place + 1)) + (groups - 1 - own), groups)
        load(values.at[slot], held.at[place]).start()
        if len(sources) == 1:
            load(sources[0], blocks.at[place]).start()
            continue
        inner, outer = sources
        if inner.shape[0] != rows:
            picked = pl.multiple_of(far_table[0, own] * rows, rows)
            inner = inner.at[pl.ds(picked, rows), :]
        near = pltpu.make_async_copy(inner, blocks.at[place], sems.at[len(loads)])
        copy = load(outer, blocks.at[place])
        deep = is_inner(groups)

        @pl.when(deep)
        def _():
            near.start()

        @pl.when(jnp.logical_not(deep))
        def _():
            copy.start()

    return loads


def add_cross(groups, total, dst_block, held, blocks, loads):
    own = lax.axis_index("group")
    for place in range(groups - 1):
        slot = lax.rem((own ^ (place + 1)) + (groups - 1 - own), groups)
        loads[2 * place].wait()
        loads[2 * place + 1].wait()
        total[dst_block[0, slot]] += turned_dot(held[place], blocks[place])


def split_received(plan, refs):
    received = []
    for count in plan:
        received.append(refs[:count])
        refs = refs[count:]
    return received, refs


def relay_kernel(rows, far_table, raw, *rest):
    *outs, sems = rest
    own = lax.axis_index("group")
    copies = []
    for i, (peer, out) in enumerate(zip((1, 2, 3), outs)):
        block = far_table[0, own ^ peer]
        source = raw.at[pl.ds(pl.multiple_of(block * rows, rows), rows), :]
        copies.append(pltpu.make_async_copy(source, out, sems.at[i]))
        copies[-1].start()
    for copy in copies:
        copy.wait()


def middle_kernel(
    rows, plan, send_group, send_member, dst_block, far_table, base, slope, weight, values, after, *rest
):
    received, rest = split_received(plan, rest)
    cross = len(plan)
    carry_out, pull_out, back_out, *outs, held, blocks, sems, send_sems = rest
    loads = fetch_cross(rows, cross + 1, far_table, received, blocks, values, held, sems)
    carry_out[...] = base[...]
    add_cross(cross + 1, carry_out, dst_block, held, blocks, loads)
    for block in range(carry_out.shape[0]):
        part = pl.ds(block * rows, rows)
        pull = (carry_out[block] * slope[part, :]).astype(BF16)
        pull_out[part, :] = pull
        back_out[part, :] = times_transpose(pull, weight[...]).astype(BF16)
    for copy in start_sends(back_out, send_group, send_member, outs[:cross], outs[cross:], send_sems, rows):
        copy.wait()


def last_kernel(rows, plan, dst_block, far_table, base, values, after, *rest):
    received, (out, total, held, blocks, sems) = split_received(plan, rest)
    loads = fetch_cross(rows, len(plan) + 1, far_table, received, blocks, values, held, sems)
    total[...] = base[...]
    add_cross(len(plan) + 1, total, dst_block, held, blocks, loads)
    out[...] = total[...].reshape(out.shape).astype(BF16)


def params():
    return pltpu.CompilerParams(vmem_limit_bytes=LIMIT)


def send_shapes(rows, width, count):
    return [jax.ShapeDtypeStruct((rows, width), BF16)] * count


def relayed(groups):
    return groups == 4 * PAIR


def group_exchange(rows, back, group_sends, far_table):
    groups = lax.axis_size("group")
    line = relayed(groups)

    def inner(g):
        return 0 < g // PAIR < groups // PAIR - 1

    def permute(block, peer, keep=lambda g: True):
        return lax.ppermute(block, "group", [(g, g ^ peer) for g in range(groups) if keep(g)])

    if not line:
        return [[permute(block, peer)] for peer, block in enumerate(group_sends, 1)]
    raw = permute(back, 6, inner)
    near = {peer: permute(group_sends[peer - 1], peer) for peer in (2, 3)}
    far = {peer: permute(group_sends[peer - 1], peer, lambda g: not inner(g)) for peer in (6, 7, 4, 5)}
    sibling = permute(group_sends[0], 1)
    to_sibling, to_same, to_cross = pl.pallas_call(
        functools.partial(relay_kernel, rows),
        out_shape=send_shapes(rows, back.shape[1], 3),
        in_specs=[SMEM, ANY],
        out_specs=[ANY] * 3,
        scratch_shapes=[pltpu.SemaphoreType.DMA((3,))],
        compiler_params=params(),
        name="relay_pick",
    )(far_table, raw)
    same = permute(to_same, 2, inner)
    cross = permute(to_cross, 3, inner)
    swapped = permute(to_sibling, 1, inner)
    return [
        [sibling],
        [near[2]],
        [near[3]],
        [far[4], same],
        [far[5], cross],
        [raw, far[6]],
        [swapped, far[7]],
    ]


def member_exchange(member_sends, capacity):
    members = lax.axis_size("member")
    return [
        lax.ppermute(block, "member", [(m, (m + 1 + place // capacity) % members) for m in range(members)])
        for place, block in enumerate(member_sends)
    ]


def stage_peers(axis, stride, size):
    total = lax.axis_size(axis)
    perms = [[(i, i ^ (s * stride)) for i in range(total)] for s in range(1, size)]
    return lax.axis_index(axis) // stride % size, perms


def kernel_call(kernel, out_shape, operands, scratch=(), outs_any=False):
    return pl.pallas_call(
        kernel,
        out_shape=out_shape,
        in_specs=[VMEM] * len(operands),
        out_specs=jax.tree.map(lambda _: ANY if outs_any else VMEM, out_shape),
        scratch_shapes=list(scratch),
        compiler_params=params(),
    )(*operands)


def part_kernel(agg, pull, keep, give):
    place = lax.rem(lax.axis_index("group"), PAIR)
    half = keep.shape[0]
    for number in range(PAIR):
        part = turned_dot(agg[:, number * half : (number + 1) * half], pull[...])

        @pl.when(place == number)
        def _():
            keep[...] = part

        @pl.when(place != number)
        def _():
            give[...] = part.astype(BF16)


def split_kernel(keep, got, own, *gives):
    place = lax.axis_index("member")
    size = own.shape[0]
    for number, out in enumerate((own,) + gives):
        part = pl.ds(pl.multiple_of((place ^ number) * size, size), size)
        out[...] = (keep[part, :] + got[part, :].astype(F32)).astype(out.dtype)


def join_kernel(*refs):
    *pieces, out = refs
    place = lax.axis_index("member")
    size = pieces[0].shape[0]
    for number, piece in enumerate(pieces):
        out[pl.ds(pl.multiple_of((place ^ number) * size, size), size), :] = piece[...]


def finish_kernel(scale, *refs):
    *pieces, out = refs
    place = lax.rem(lax.axis_index("group"), PAIR)
    size = pieces[0].shape[0]
    for number, piece in enumerate(pieces):
        out[pl.ds(pl.multiple_of((place ^ number) * size, size), size), :] = piece[...].astype(F32) * scale


def pairwise(parts):
    while len(parts) > 1:
        parts = [left + right for left, right in zip(parts[0::2], parts[1::2])]
    return parts[0]


def weight_total(aggregate, pulled, scale):
    groups, members = lax.axis_size("group"), lax.axis_size("member")
    width, depth = aggregate.shape[1], pulled.shape[1]
    half, piece = width // PAIR, width // PAIR // members
    _, pair_perms = stage_peers("group", 1, PAIR)
    _, member_perms = stage_peers("member", 1, members)
    _, line_perms = stage_peers("group", PAIR, groups // PAIR)

    def permute(blocks, axis, perms):
        return [lax.ppermute(block, axis, perm) for block, perm in zip(blocks, perms)]

    def shape(rows, dtype):
        return jax.ShapeDtypeStruct((rows, depth), dtype)

    keep, give = kernel_call(part_kernel, [shape(half, F32), shape(half, BF16)], (aggregate, pulled))
    (got,) = permute([give], "group", pair_perms)
    own, *gives = kernel_call(split_kernel, [shape(piece, F32)] + [shape(piece, BF16)] * (members - 1), (keep, got))
    got = permute(gives, "member", member_perms)
    total = sum((block.astype(F32) for block in got), own).astype(BF16)
    got = permute([total] * (groups // PAIR - 1), "group", line_perms)
    total = pairwise([block.astype(F32) for block in [total] + got]).astype(BF16)
    got = permute([total] * (members - 1), "member", member_perms)
    total = kernel_call(join_kernel, shape(half, BF16), [total] + got)
    got = permute([total], "group", pair_perms)
    return kernel_call(functools.partial(finish_kernel, scale), shape(width, F32), [total] + got)


def body(
    agg_one,
    agg_two,
    grad_out,
    hop_one_weight,
    hop_two_weight,
    block_values,
    src_slot,
    dst_block,
    block_count,
    send_member,
    send_group,
):
    groups, members = lax.axis_size("group"), lax.axis_size("member")
    labels, width = agg_one.shape
    _, rows = block_values.shape[:2]
    local = labels // rows
    capacity = send_member.shape[2]
    cross = groups - 1
    peers = (members - 1) * capacity
    grad_scale = float(labels * members * groups) ** (-0.5)

    field = jax.ShapeDtypeStruct((labels, width), BF16)
    total = jax.ShapeDtypeStruct((local, rows, width), F32)
    sends = send_shapes(rows, width, cross + peers)
    send_sems = pltpu.SemaphoreType.DMA((cross + peers,))
    cross_scratch = [
        pltpu.VMEM((cross, rows, rows), BF16),
        pltpu.VMEM((cross, rows, width), BF16),
    ]

    def sweep(back, base, received):
        return pl.pallas_call(
            functools.partial(sweep_kernel, rows, cross),
            out_shape=total,
            in_specs=[SMEM, SMEM, SMEM, SMEM, ANY, VMEM, VMEM] + [ANY] * peers,
            out_specs=VMEM,
            scratch_shapes=[
                pltpu.VMEM((local + members * capacity, rows, width), BF16),
                pltpu.SemaphoreType.DMA((local + members * capacity,)),
            ],
            compiler_params=params(),
            name="sweep",
        )(src_slot, dst_block, block_count, send_member, back, base, block_values, *received)

    plan = [1, 1, 1, 2, 2, 2, 2] if relayed(groups) else [1] * cross

    far_table = send_group
    if relayed(groups):
        far_table = lax.ppermute(send_group, "group", [(g, g ^ 6) for g in range(groups)])
    pull_two, back_two, *outs = pl.pallas_call(
        functools.partial(first_kernel, rows, cross),
        out_shape=[field, field] + sends,
        in_specs=[SMEM, SMEM, VMEM, VMEM, VMEM],
        out_specs=[VMEM, VMEM] + [ANY] * (cross + peers),
        scratch_shapes=[send_sems],
        compiler_params=params(),
        name="first",
    )(send_group, send_member, agg_two, hop_two_weight, grad_out)
    from_group = group_exchange(rows, back_two, outs[:cross], far_table)
    from_member = member_exchange(outs[cross:], capacity)
    slope_one = silu_slope(jnp.dot(agg_one, hop_one_weight, preferred_element_type=F32))
    grad_w_two = weight_total(agg_two, pull_two, grad_scale)
    base_two = sweep(back_two, grad_out, from_member)

    carry, pull_one, back_one, *outs = pl.pallas_call(
        functools.partial(middle_kernel, rows, plan),
        out_shape=[total, field, field] + sends,
        in_specs=[SMEM] * 4 + [VMEM] * 3 + [ANY] * (2 + sum(plan)),
        out_specs=[VMEM, VMEM, VMEM] + [ANY] * (cross + peers),
        scratch_shapes=cross_scratch + [pltpu.SemaphoreType.DMA((2 * cross,)), send_sems],
        compiler_params=params(),
        name="middle",
    )(
        *(send_group, send_member, dst_block, far_table, base_two, slope_one),
        *(hop_one_weight, block_values, grad_w_two),
        *sum(from_group, []),
    )
    from_group = group_exchange(rows, back_one, outs[:cross], far_table)
    from_member = member_exchange(outs[cross:], capacity)
    grad_w_one = weight_total(agg_one, pull_one, grad_scale)
    base_one = sweep(back_one, carry, from_member)

    grad_emb = pl.pallas_call(
        functools.partial(last_kernel, rows, plan),
        out_shape=field,
        in_specs=[SMEM] * 2 + [VMEM] + [ANY] * (2 + sum(plan)),
        out_specs=VMEM,
        scratch_shapes=[pltpu.VMEM((local, rows, width), F32)]
        + cross_scratch
        + [pltpu.SemaphoreType.DMA((2 * cross,))],
        compiler_params=params(),
        name="last",
    )(dst_block, far_table, base_one, block_values, grad_w_one, *sum(from_group, []))
    return (grad_emb, grad_w_one, grad_w_two)


def solution(mesh):
    in_specs = (
        P(("member", "group"), None),
        P(("member", "group"), None),
        P(("member", "group"), None),
        P(),
        P(),
        P(("member", "group"), None, None),
        P(("member", "group"), None),
        P(("member", "group"), None),
        P(("member", "group")),
        P(("member", "group"), None, None),
        P(("member", "group"), None),
    )
    out_specs = (P(("member", "group"), None), P(), P())
    return jax.shard_map(body, mesh=mesh, in_specs=in_specs, out_specs=out_specs, check_vma=False)
```

```python
import functools

import jax
import jax.numpy as jnp
from jax import lax
from jax.experimental import pallas as pl
from jax.experimental.pallas import tpu as pltpu
from jax.sharding import PartitionSpec as P


F32 = jnp.float32
BF16 = jnp.bfloat16
VMEM = pl.BlockSpec(memory_space=pltpu.VMEM)
SMEM = pl.BlockSpec(memory_space=pltpu.SMEM)
ANY = pl.BlockSpec(memory_space=pl.ANY)
LIMIT = 20 << 20
PAIR = 2


def silu_slope(value):
    sig = jax.nn.sigmoid(value)
    return sig * (1.0 + value * (1.0 - sig))


def turned_dot(values, rows):
    return lax.dot_general(values, rows, (((0,), (0,)), ((), ())), preferred_element_type=F32)


def times_transpose(left, weight):
    return lax.dot_general(left, weight, (((1,), (1,)), ((), ())), preferred_element_type=F32)


def start_sends(back, ready, send_group, send_member, outs, cross, sems, rows):
    members, capacity = send_member.shape[1], send_member.shape[2]
    own_group, own_member = lax.axis_index("group"), lax.axis_index("member")
    source = back.at[pl.ds(ready * rows, rows), :]
    copies = []
    for number, out in enumerate(outs):
        if number < cross:
            block = send_group[0, own_group ^ (number + 1)]
        else:
            shift, which = 1 + (number - cross) // capacity, (number - cross) % capacity
            block = send_member[0, lax.rem(own_member + shift, members), which]
        copies.append(pltpu.make_async_copy(source, out, sems.at[number]))

        @pl.when(block == ready)
        def _():
            copies[-1].start()

    return copies


def first_kernel(rows, cross, send_group, send_member, agg, weight, grad, pull_out, back_out, *rest):
    *outs, sems = rest
    copies = []
    for block in range(agg.shape[0] // rows):
        part = pl.ds(block * rows, rows)
        lift = jnp.dot(agg[part, :], weight[...], preferred_element_type=F32)
        pull = (grad[part, :].astype(F32) * silu_slope(lift)).astype(BF16)
        pull_out[part, :] = pull
        back_out[part, :] = times_transpose(pull, weight[...]).astype(BF16)
        copies = start_sends(back_out, block, send_group, send_member, outs, cross, sems, rows)
    for copy in copies:
        copy.wait()


def sweep_kernel(
    rows, groups, places, plan, src_slot, dst_block, block_count, send_member, far_table, back, base, values, *rest
):
    early, rest = split_received(plan, rest)
    *received, total, pool, held, blocks, sems, early_sems = rest
    members, capacity = send_member.shape[1], send_member.shape[2]
    local = back.shape[0] // rows
    own = lax.axis_index("member")
    copies = []

    def fill(source, slot):
        copies.append(pltpu.make_async_copy(source, pool.at[slot], sems.at[len(copies)]))
        copies[-1].start()

    for block in range(local):
        fill(back.at[pl.ds(block * rows, rows), :], block)
    for which in range(capacity):
        block = send_member[0, own, which]
        fill(back.at[pl.ds(pl.multiple_of(block * rows, rows), rows), :], local + own * capacity + which)
    for place, source in enumerate(received):
        shift, which = 1 + place // capacity, place % capacity
        peer = lax.rem(own + (members - shift), members)
        fill(source, local + peer * capacity + which)
    loads = fetch_cross(rows, groups, places, far_table, early, blocks, values, held, early_sems)
    total[...] = base[...].astype(F32).reshape(total.shape)
    for copy in copies:
        copy.wait()

    def step(slot, carry):
        total[dst_block[0, slot]] += turned_dot(values[slot], pool[src_slot[0, slot]])
        return carry

    lax.fori_loop(groups - 1, block_count[0], step, 0)
    add_cross(groups, places, total, dst_block, held, blocks, loads)


def is_inner(groups):
    chip = lax.axis_index("group") // PAIR
    return (chip > 0) & (chip < groups // PAIR - 1)


def slot_of(place, groups):
    own = lax.axis_index("group")
    return lax.rem((own ^ (place + 1)) + (groups - 1 - own), groups)


def fetch_cross(rows, groups, places, far_table, received, blocks, values, held, sems):
    own = lax.axis_index("group")
    loads = []
    for number, (place, sources) in enumerate(zip(places, received)):
        value_sem, block_sem, to = sems.at[2 * number], sems.at[2 * number + 1], blocks.at[number]
        loads.append(pltpu.make_async_copy(values.at[slot_of(place, groups)], held.at[number], value_sem))
        loads[-1].start()
        loads.append(pltpu.make_async_copy(sources[-1], to, block_sem))
        if len(sources) == 1:
            loads[-1].start()
            continue
        inner = sources[0]
        if inner.shape[0] != rows:
            picked = pl.multiple_of(far_table[0, own] * rows, rows)
            inner = inner.at[pl.ds(picked, rows), :]
        deep = is_inner(groups)

        @pl.when(deep)
        def _():
            pltpu.make_async_copy(inner, to, block_sem).start()

        @pl.when(jnp.logical_not(deep))
        def _():
            loads[-1].start()

    return loads


def add_cross(groups, places, total, dst_block, held, blocks, loads):
    for number, place in enumerate(places):
        loads[2 * number].wait()
        loads[2 * number + 1].wait()
        total[dst_block[0, slot_of(place, groups)]] += turned_dot(held[number], blocks[number])


def split_received(plan, refs):
    received = []
    for count in plan:
        received.append(refs[:count])
        refs = refs[count:]
    return received, refs


def relay_kernel(rows, far_table, raw, *rest):
    *outs, sems = rest
    own = lax.axis_index("group")
    copies = []
    for i, (peer, out) in enumerate(zip((1, 2, 3), outs)):
        block = far_table[0, own ^ peer]
        source = raw.at[pl.ds(pl.multiple_of(block * rows, rows), rows), :]
        copies.append(pltpu.make_async_copy(source, out, sems.at[i]))
        copies[-1].start()
    for copy in copies:
        copy.wait()


def middle_kernel(
    rows, groups, places, plan, send_group, send_member, dst_block, far_table, base, slope, weight, values, *rest
):
    received, rest = split_received(plan, rest)
    carry_out, pull_out, back_out, *outs, held, blocks, sems, send_sems = rest
    loads = fetch_cross(rows, groups, places, far_table, received, blocks, values, held, sems)
    carry_out[...] = base[...]
    add_cross(groups, places, carry_out, dst_block, held, blocks, loads)
    copies = []
    for block in range(carry_out.shape[0]):
        part = pl.ds(block * rows, rows)
        pull = (carry_out[block] * slope[part, :]).astype(BF16)
        pull_out[part, :] = pull
        back_out[part, :] = times_transpose(pull, weight[...]).astype(BF16)
        copies = start_sends(back_out, block, send_group, send_member, outs, groups - 1, send_sems, rows)
    for copy in copies:
        copy.wait()


def last_kernel(
    rows, groups, places, plan, scale, dst_block, far_table, base, own_half, sibling_half, values, after, *rest
):
    received, (out, grad, total, held, blocks, sems) = split_received(plan, rest)
    loads = fetch_cross(rows, groups, places, far_table, received, blocks, values, held, sems)
    total[...] = base[...]
    finish_kernel(scale, own_half, sibling_half, grad)
    add_cross(groups, places, total, dst_block, held, blocks, loads)
    out[...] = total[...].reshape(out.shape).astype(BF16)


def params():
    return pltpu.CompilerParams(vmem_limit_bytes=LIMIT)


def send_shapes(rows, width, count):
    return [jax.ShapeDtypeStruct((rows, width), BF16)] * count


def relayed(groups):
    return groups == 4 * PAIR


def group_exchange(rows, back, group_sends, far_table):
    groups = lax.axis_size("group")
    line = relayed(groups)

    def inner(g):
        return 0 < g // PAIR < groups // PAIR - 1

    def permute(block, peer, keep=lambda g: True):
        return lax.ppermute(block, "group", [(g, g ^ peer) for g in range(groups) if keep(g)])

    if not line:
        return [[permute(block, peer)] for peer, block in enumerate(group_sends, 1)]
    raw = permute(back, 6, inner)
    near = {peer: permute(group_sends[peer - 1], peer) for peer in (2, 3)}
    far = {peer: permute(group_sends[peer - 1], peer, lambda g: not inner(g)) for peer in (6, 7, 4, 5)}
    sibling = permute(group_sends[0], 1)
    to_sibling, to_same, to_cross = pl.pallas_call(
        functools.partial(relay_kernel, rows),
        out_shape=send_shapes(rows, back.shape[1], 3),
        in_specs=[SMEM, ANY],
        out_specs=[ANY] * 3,
        scratch_shapes=[pltpu.SemaphoreType.DMA((3,))],
        compiler_params=params(),
        name="relay_pick",
    )(far_table, raw)
    same = permute(to_same, 2, inner)
    cross = permute(to_cross, 3, inner)
    swapped = permute(to_sibling, 1, inner)
    return [
        [sibling],
        [near[2]],
        [near[3]],
        [far[4], same],
        [far[5], cross],
        [raw, far[6]],
        [swapped, far[7]],
    ]


def member_exchange(member_sends, capacity):
    members = lax.axis_size("member")
    return [
        lax.ppermute(block, "member", [(m, (m + 1 + place // capacity) % members) for m in range(members)])
        for place, block in enumerate(member_sends)
    ]


def stage_peers(axis, stride, size):
    total = lax.axis_size(axis)
    perms = [[(i, i ^ (s * stride)) for i in range(total)] for s in range(1, size)]
    return lax.axis_index(axis) // stride % size, perms


def kernel_call(kernel, out_shape, operands, scratch=(), outs_any=False):
    return pl.pallas_call(
        kernel,
        out_shape=out_shape,
        in_specs=[VMEM] * len(operands),
        out_specs=jax.tree.map(lambda _: ANY if outs_any else VMEM, out_shape),
        scratch_shapes=list(scratch),
        compiler_params=params(),
    )(*operands)


def part_kernel(agg, pull, keep, give):
    place = lax.rem(lax.axis_index("group"), PAIR)
    half = keep.shape[0]
    for number in range(PAIR):
        part = turned_dot(agg[:, number * half : (number + 1) * half], pull[...])

        @pl.when(place == number)
        def _():
            keep[...] = part

        @pl.when(place != number)
        def _():
            give[...] = part.astype(BF16)


def split_kernel(keep, got, own, *gives):
    place = lax.axis_index("member")
    size = own.shape[0]
    for number, out in enumerate((own,) + gives):
        part = pl.ds(pl.multiple_of((place ^ number) * size, size), size)
        out[...] = (keep[part, :] + got[part, :].astype(F32)).astype(out.dtype)


def join_kernel(*refs):
    *pieces, out = refs
    place = lax.axis_index("member")
    size = pieces[0].shape[0]
    for number, piece in enumerate(pieces):
        out[pl.ds(pl.multiple_of((place ^ number) * size, size), size), :] = piece[...]


def finish_kernel(scale, *refs):
    *pieces, out = refs
    place = lax.rem(lax.axis_index("group"), PAIR)
    size = pieces[0].shape[0]
    for number, piece in enumerate(pieces):
        out[pl.ds(pl.multiple_of((place ^ number) * size, size), size), :] = piece[...].astype(F32) * scale


def pairwise(parts):
    while len(parts) > 1:
        parts = [left + right for left, right in zip(parts[0::2], parts[1::2])]
    return parts[0]


def stage(blocks, axis, stride, size):
    _, perms = stage_peers(axis, stride, size)
    return [lax.ppermute(block, axis, perm) for block, perm in zip(blocks, perms)]


def weight_piece(aggregate, pulled):
    groups, members = lax.axis_size("group"), lax.axis_size("member")
    width, depth = aggregate.shape[1], pulled.shape[1]
    half, piece = width // PAIR, width // PAIR // members

    def shape(rows, dtype):
        return jax.ShapeDtypeStruct((rows, depth), dtype)

    keep, give = kernel_call(part_kernel, [shape(half, F32), shape(half, BF16)], (aggregate, pulled))
    (got,) = stage([give], "group", 1, PAIR)
    own, *gives = kernel_call(split_kernel, [shape(piece, F32)] + [shape(piece, BF16)] * (members - 1), (keep, got))
    got = stage(gives, "member", 1, members)
    total = sum((block.astype(F32) for block in got), own).astype(BF16)
    got = stage([total] * (groups // PAIR - 1), "group", PAIR, groups // PAIR)
    return pairwise([block.astype(F32) for block in [total] + got]).astype(BF16)


def weight_halves(total):
    members = lax.axis_size("member")
    got = stage([total] * (members - 1), "member", 1, members)
    shape = jax.ShapeDtypeStruct((members * total.shape[0], total.shape[1]), BF16)
    half = kernel_call(join_kernel, shape, [total] + got)
    return [half] + stage([half], "group", 1, PAIR)


def body(
    agg_one,
    agg_two,
    grad_out,
    hop_one_weight,
    hop_two_weight,
    block_values,
    src_slot,
    dst_block,
    block_count,
    send_member,
    send_group,
):
    groups, members = lax.axis_size("group"), lax.axis_size("member")
    labels, width = agg_one.shape
    _, rows = block_values.shape[:2]
    local = labels // rows
    capacity = send_member.shape[2]
    cross = groups - 1
    peers = (members - 1) * capacity
    grad_scale = float(labels * members * groups) ** (-0.5)

    field = jax.ShapeDtypeStruct((labels, width), BF16)
    total = jax.ShapeDtypeStruct((local, rows, width), F32)
    square = jax.ShapeDtypeStruct(hop_one_weight.shape, F32)
    sends = send_shapes(rows, width, cross + peers)
    send_sems = pltpu.SemaphoreType.DMA((cross + peers,))
    plan = [1, 1, 1, 2, 2, 2, 2] if relayed(groups) else [1] * cross
    late = (3, 4) if relayed(groups) else tuple(range(cross))
    early = tuple(place for place in range(cross) if place not in late)
    early_plan, late_plan = [plan[place] for place in early], [plan[place] for place in late]

    def cross_scratch(places):
        count = max(len(places), 1)
        return [
            pltpu.VMEM((count, rows, rows), BF16),
            pltpu.VMEM((count, rows, width), BF16),
        ], pltpu.SemaphoreType.DMA((2 * count,))

    def pick(blocks, places):
        return sum((blocks[place] for place in places), [])

    def sweep(back, base, from_group, received):
        scratch, sems = cross_scratch(early)
        return pl.pallas_call(
            functools.partial(sweep_kernel, rows, groups, early, early_plan),
            out_shape=total,
            in_specs=[SMEM] * 5 + [ANY] + [VMEM] * 2 + [ANY] * (sum(early_plan) + peers),
            out_specs=VMEM,
            scratch_shapes=[pltpu.VMEM((local + members * capacity, rows, width), BF16)]
            + scratch
            + [pltpu.SemaphoreType.DMA((local + members * capacity,)), sems],
            compiler_params=params(),
            name="sweep",
        )(
            *(src_slot, dst_block, block_count, send_member, far_table, back, base, block_values),
            *pick(from_group, early),
            *received,
        )

    scratch, sems = cross_scratch(late)
    far_table = send_group
    if relayed(groups):
        far_table = lax.ppermute(send_group, "group", [(g, g ^ 6) for g in range(groups)])
    pull_two, back_two, *outs = pl.pallas_call(
        functools.partial(first_kernel, rows, cross),
        out_shape=[field, field] + sends,
        in_specs=[SMEM, SMEM, VMEM, VMEM, VMEM],
        out_specs=[VMEM, VMEM] + [ANY] * (cross + peers),
        scratch_shapes=[send_sems],
        compiler_params=params(),
        name="first",
    )(send_group, send_member, agg_two, hop_two_weight, grad_out)
    from_group = group_exchange(rows, back_two, outs[:cross], far_table)
    from_member = member_exchange(outs[cross:], capacity)
    slope_one = silu_slope(jnp.dot(agg_one, hop_one_weight, preferred_element_type=F32))
    piece_two = weight_piece(agg_two, pull_two)
    base_two = sweep(back_two, grad_out, from_group, from_member)
    carry, pull_one, back_one, *outs = pl.pallas_call(
        functools.partial(middle_kernel, rows, groups, late, late_plan),
        out_shape=[total, field, field] + sends,
        in_specs=[SMEM] * 4 + [VMEM] * 3 + [ANY] * (1 + sum(late_plan)),
        out_specs=[VMEM, VMEM, VMEM] + [ANY] * (cross + peers),
        scratch_shapes=scratch + [sems, send_sems],
        compiler_params=params(),
        name="middle",
    )(
        *(send_group, send_member, dst_block, far_table, base_two, slope_one),
        *(hop_one_weight, block_values),
        *pick(from_group, late),
    )

    from_group = group_exchange(rows, back_one, outs[:cross], far_table)
    from_member = member_exchange(outs[cross:], capacity)
    halves_two = weight_halves(piece_two)
    halves_one = weight_halves(weight_piece(agg_one, pull_one))
    base_one = sweep(back_one, carry, from_group, from_member)
    grad_w_two = kernel_call(functools.partial(finish_kernel, grad_scale), square, halves_two)

    grad_emb, grad_w_one = pl.pallas_call(
        functools.partial(last_kernel, rows, groups, late, late_plan, grad_scale),
        out_shape=[field, square],
        in_specs=[SMEM] * 2 + [VMEM] * 3 + [ANY] * (2 + sum(late_plan)),
        out_specs=[VMEM, VMEM],
        scratch_shapes=[pltpu.VMEM((local, rows, width), F32)] + scratch + [sems],
        compiler_params=params(),
        name="last",
    )(dst_block, far_table, base_one, *halves_one, block_values, grad_w_two, *pick(from_group, late))
    return (grad_emb, grad_w_one, grad_w_two)


def solution(mesh):
    in_specs = (
        P(("member", "group"), None),
        P(("member", "group"), None),
        P(("member", "group"), None),
        P(),
        P(),
        P(("member", "group"), None, None),
        P(("member", "group"), None),
        P(("member", "group"), None),
        P(("member", "group")),
        P(("member", "group"), None, None),
        P(("member", "group"), None),
    )
    out_specs = (P(("member", "group"), None), P(), P())
    return jax.shard_map(body, mesh=mesh, in_specs=in_specs, out_specs=out_specs, check_vma=False)
```
